32 devices in a mesh: groups: 2 (over x), gx: 16 (over z, y, core).
Axes of the slice: x: 2, y: 2, z: 4, core: 2. Of those that a mesh axis runs over, the one named last changes fastest.
Arguments:
- hidden: bfloat16 [39936, 768], P('gx', 'groups'), parts along dimension 1, may hold values from -6 to 6
- residual: bfloat16 [16384, 768], P('gx', 'groups'), parts along dimension 1, may hold values from -120 to 120
- w_down: bfloat16 [16, 19968, 2048], P('gx'), may hold values from -0.03125 to 0.03125
- gain: bfloat16 [16384], P('gx'), may hold values from 0.099609375 to 1.8984375
- w_qkv: bfloat16 [16, 2048, 5120], P('gx'), may hold values from -0.046875 to 0.046875
Outputs:
- stream: bfloat16 [16384, 768], P('gx', 'groups'), parts along dimension 1
- qkv: bfloat16 [10240, 768], P('gx', 'groups'), parts along dimension 1
The draws below stay inside these ranges and needn't reach their ends.
There are 2 independent parts, one for each index of `groups`. The reference program is written for one: setup_inputs(seed, part) draws one part's arguments, and reference() takes and returns one part's arrays. A program takes and returns all parts, laid end to end along the dimension named above; an argument that names none is the same for every part. Nothing has to cross between parts.
All inputs are finite; a program needn't handle non-finite values.
Results may differ from the reference program's by a relative error of at most 0.0058.
Values may be sent and summed in bfloat16 or wider, within the bound.
No kernel may reach another device: no remote copies, remote signals or barrier semaphores. Data moves between devices by JAX's collectives and lax.ppermute only.
A program may use at most 192 MiB of HBM per device.

```python
import jax
import jax.numpy as jnp
from jax import lax

D = 16384
FFN_WIN = 39936
TOKENS = 384
XS = 8
YS = 2
QKV = 10240
N_GX = 16


def draw_residual(key, part):
    first, second, third = jax.random.split(jax.random.fold_in(key, 7), 3)
    position = jnp.arange(D, dtype=jnp.float32)[:, None] / D
    feature_scale = jnp.exp(jax.random.uniform(first, (D, 1), jnp.float32, jnp.log(0.3), jnp.log(3.0)))
    base = jnp.clip(jax.random.normal(second, (D, TOKENS), jnp.float32), -6.0, 6.0)
    ramp = jnp.sqrt(0.5 + position)
    token_scale = jnp.exp(jax.random.uniform(third, (1, TOKENS), jnp.float32, jnp.log(0.4), jnp.log(4.0)))
    return (base * feature_scale * ramp * token_scale).astype(jnp.bfloat16)


def block_levels(stream_key, extent, cuts, least, high):
    loudness = 1.0
    for dim, parts in cuts:
        steps = jax.random.uniform(jax.random.fold_in(jax.random.fold_in(stream_key, 6), dim), (parts,), jnp.float32, least / len(cuts), high / len(cuts))
        loudness = loudness * jnp.repeat(jnp.exp(steps), extent[dim] // parts).reshape((-1,) + (1,) * (len(extent) - 1 - dim))
    return loudness


def gaussian(rng, shape, scale, most, cuts=(), kind=jnp.bfloat16):
    level = block_levels(rng, shape, cuts, -0.22, 0.18) if cuts else 1.0
    result = jax.random.normal(rng, shape, jnp.float32) * scale * level
    return jnp.minimum(jnp.maximum(result, -most), most).astype(kind)


def setup_inputs(seed: int = 0, part: int = 0) -> dict:
    keys = jax.random.split(jax.random.key(seed), 6)
    part_keys = jax.random.split(jax.random.fold_in(keys[5], part), 6)
    hidden = gaussian(part_keys[0], (FFN_WIN, TOKENS), 1.0, 6.0, ((0, 16),))
    residual = draw_residual(jax.random.fold_in(jax.random.fold_in(keys[5], part), 71), part)
    w_down = gaussian(keys[2], (N_GX, FFN_WIN // YS, D // XS), FFN_WIN ** -0.5, 0.03125, ((0, 16),))
    gain = jnp.clip(1.0 + 0.18 * jax.random.normal(keys[3], (D,), jnp.float32), 0.099609375, 1.8984375).astype(jnp.bfloat16)
    w_qkv = gaussian(keys[4], (N_GX, D // XS, QKV // YS), D ** -0.5, 0.046875, ((0, 16),))
    return dict(hidden=hidden, residual=residual, w_down=w_down, gain=gain, w_qkv=w_qkv)


def reference(hidden, residual, w_down, gain, w_qkv):
    down_full = w_down.reshape(XS, YS, XS, FFN_WIN // N_GX, D // XS)
    down_full = down_full.transpose(2, 1, 3, 0, 4).reshape(FFN_WIN, D)
    qkv_full = w_qkv.reshape(XS, YS, D // XS, XS, QKV // N_GX)
    qkv_full = qkv_full.transpose(0, 2, 3, 1, 4).reshape(D, QKV)
    down = jnp.dot(down_full.T, hidden, preferred_element_type=jnp.float32)
    stream = (residual.astype(jnp.float32) + down).astype(jnp.bfloat16)
    values = stream.astype(jnp.float32)
    sumsq = lax.optimization_barrier(jnp.sum(values * values, axis=0))
    inv_rms = lax.rsqrt(sumsq / D + 1e-05)
    normed = (values * gain.astype(jnp.float32)[:, None] * inv_rms[None, :]).astype(jnp.bfloat16)
    qkv = jnp.dot(qkv_full.T, normed, preferred_element_type=jnp.float32).astype(jnp.bfloat16)
    return (stream, qkv)
```

```python
import jax
import jax.numpy as jnp
from jax import lax
from jax.sharding import PartitionSpec as P

D = 16384
XS = 8
LANES = 128


def block_at(place):
    half = XS // 2
    return jnp.where(place < half, 2 * place, 2 * (XS - 1 - place) + 1)


def place_of(block):
    return jnp.where(block % 2 == 0, block // 2, XS - 1 - block // 2)


def static_block_at(place):
    return 2 * place if place < XS // 2 else 2 * (XS - 1 - place) + 1


def moved(value, ys, by):
    route = []
    for place in range(XS):
        source = static_block_at(place)
        target = static_block_at((place + by) % XS)
        for low in range(ys):
            route.append((source * ys + low, target * ys + low))
    return lax.ppermute(value, "gx", route)


def swapped(value, stride):
    count = lax.axis_size("gx")
    return lax.ppermute(value, "gx", [(low, low ^ 1 << stride) for low in range(count)])


def token_groups(tokens):
    if tokens % (3 * LANES) == 0:
        return [tokens * 2 // 3, tokens // 3]
    return [tokens]


def on_device(hidden, residual, w_down, gain, w_qkv):
    dev_index = lax.axis_index("gx")
    ys = lax.axis_size("gx") // XS
    y_bits = ys.bit_length() - 1
    x_bits = XS.bit_length() - 1
    place = place_of(dev_index // ys)
    low_index = dev_index % ys

    chunk_rows, tokens = hidden.shape
    half_rows = chunk_rows // 2
    width = w_down.shape[2]
    own_width = residual.shape[0]
    columns = w_qkv.shape[2] // XS
    down_tiles = w_down.reshape(XS * 2, half_rows, width)
    qkv_tile = w_qkv[0]

    res_t = residual.T
    gain_full = gain
    for position in range(y_bits):
        high = (dev_index >> position) % 2 == 1
        other_res, other_gain = swapped(res_t, position), swapped(gain_full, position)
        res_t = jnp.where(
            high,
            jnp.concatenate([other_res, res_t], 1),
            jnp.concatenate([res_t, other_res], 1),
        )
        gain_full = jnp.where(
            high,
            jnp.concatenate([other_gain, gain_full], 0),
            jnp.concatenate([gain_full, other_gain], 0),
        )
    gain_row = gain_full.astype(jnp.float32)[None, :]

    def down_partial(acc, piece, source_place, half):
        rows = lax.dynamic_index_in_dim(
            down_tiles, block_at(source_place % XS) * 2 + half, 0, keepdims=False
        )
        product = lax.dot_general(
            piece, rows, (((0,), (0,)), ((), ())), preferred_element_type=jnp.float32
        )
        return product if acc is None else acc + product

    sizes = token_groups(tokens)
    starts = [sum(sizes[:i]) for i in range(len(sizes))]

    streams, outs = [], []
    for start, size in zip(starts, sizes):
        pieces = [hidden[h * half_rows : (h + 1) * half_rows, start : start + size] for h in range(2)]
        acc = None
        for h in range(2):
            acc = down_partial(acc, pieces[h], place, h)
        up, down = list(pieces), list(pieces)
        for step in range(1, XS // 2 + 1):
            last = step == XS // 2
            for h in range(2):
                if not last or h == 0:
                    up[h] = moved(up[h], ys, 1)
                    acc = down_partial(acc, up[h], place + XS - step, h)
                if not last or h == 1:
                    down[h] = moved(down[h], ys, -1)
                    acc = down_partial(acc, down[h], place + step, h)
        for position in range(y_bits):
            acc = acc + swapped(acc, position)
        block = (res_t[start : start + size].astype(jnp.float32) + acc).astype(jnp.bfloat16)
        streams.append(
            lax.dynamic_slice_in_dim(block, low_index * own_width, own_width, 1).T
        )
        values = block.astype(jnp.float32)
        sumsq = jnp.sum(values * values, axis=1)
        for position in range(y_bits, y_bits + x_bits):
            sumsq = sumsq + swapped(sumsq, position)
        inv_rms = lax.rsqrt(sumsq / D + 1e-05)[:, None]
        scaled = (values * gain_row).astype(jnp.bfloat16)

        def qkv_partial(distance):
            at = block_at((place + distance) % XS) * columns
            tile = lax.dynamic_slice_in_dim(qkv_tile, at, columns, 1)
            return lax.dot_general(
                scaled, tile, (((1,), (0,)), ((), ())), preferred_element_type=jnp.float32
            )

        half = size // 2
        partials = {}
        for distance in sorted(range(XS), key=lambda d: -min(d, XS - d)):
            partials[distance] = qkv_partial(distance)
        own = partials[0]
        far = XS // 2
        sums = []
        for h in range(2):
            part = slice(h * half, (h + 1) * half)
            total = own[part]
            for by, hops in ((1, far if h == 0 else far - 1), (-1, far - 1 if h == 0 else far)):
                held = None
                for distance in range(hops, 0, -1):
                    term = partials[(by * distance) % XS][part]
                    held = term if held is None else term + held.astype(jnp.float32)
                    held = moved(held.astype(jnp.bfloat16), ys, by)
                total = total + held.astype(jnp.float32)
            sums.append(total)
        outs.append((jnp.concatenate(sums, 0) * inv_rms).astype(jnp.bfloat16).T)
    return (jnp.concatenate(streams, 1), jnp.concatenate(outs, 1))


def solution(mesh):
    placed = (
        P("gx", "groups"),
        P("gx", "groups"),
        P("gx", None, None),
        P("gx"),
        P("gx", None, None),
    )
    return jax.shard_map(
        on_device,
        mesh=mesh,
        in_specs=placed,
        out_specs=(P("gx", "groups"), P("gx", "groups")),
        check_vma=False,
    )
```

```python
import jax
import jax.numpy as jnp
from jax import lax
from jax.experimental import pallas as pl
from jax.experimental.pallas import tpu as pltpu
from jax.sharding import PartitionSpec as P


D = 16384
XS = 8
FAR = XS // 2
LANES = 128
ROOM = 8


IN_VMEM = pl.BlockSpec(memory_space=pltpu.VMEM)
IN_SMEM = pl.BlockSpec(memory_space=pltpu.SMEM)


def block_at(place):
    return jnp.where(place < FAR, 2 * place, 2 * (XS - 1 - place) + 1)


def place_of(block):
    return jnp.where(block % 2 == 0, block // 2, XS - 1 - block // 2)


def static_block_at(place):
    return 2 * place if place < FAR else 2 * (XS - 1 - place) + 1


def moved(value, ys, by):
    route = []
    for place in range(XS):
        source = static_block_at(place)
        target = static_block_at((place + by) % XS)
        for low in range(ys):
            route.append((source * ys + low, target * ys + low))
    return lax.ppermute(value, "gx", route)


def swapped(value, stride):
    count = lax.axis_size("gx")
    return lax.ppermute(value, "gx", [(low, low ^ 1 << stride) for low in range(count)])


def token_groups(tokens):
    if tokens % (3 * LANES):
        return [(0, tokens)]
    return [(0, tokens * 2 // 3), (tokens * 2 // 3, tokens)]


def down_step(table, acc, low, sides, tiles):
    count, groups = len(sides), len(sides[0][0])
    rows, width = tiles.shape[1:]
    widths = [piece.shape[1] for piece in sides[0][0]]
    size = sum(widths)
    block = min(width, 512)

    def body(table_ref, *refs):
        pieces, weights = refs[: count * groups], refs[count * groups : count * (groups + 1)]
        out, turned = refs[-2:]

        @pl.when(pl.program_id(0) == 0)
        def _():
            for j in range(count):
                start = 0
                for g in range(groups):
                    turned[j, start : start + widths[g], :] = pieces[j * groups + g][...].T
                    start += widths[g]

        total = None if acc is None else refs[count * (groups + 1)][...]
        for j in range(count):
            term = jnp.dot(turned[j], weights[j][0], preferred_element_type=jnp.float32)
            total = term if total is None else total + term
        out[...] = total

    def piece_spec(tokens):
        return pl.BlockSpec((rows, tokens), lambda i, table: (0, 0), pipeline_mode=pl.Buffered(1))

    def weight_spec(distance):
        at = distance % XS
        return pl.BlockSpec((1, rows, block), lambda i, table: (table[at], 0, i))

    in_specs = [piece_spec(tokens) for _ in sides for tokens in widths]
    in_specs += [weight_spec(far) for _, far in sides]
    operands = [piece for pieces, _ in sides for piece in pieces] + [tiles] * count
    if acc is not None:
        in_specs.append(pl.BlockSpec((size, block), lambda i, table: (low // size, i)))
        operands.append(acc)
    need = count * (4 * rows * size + 4 * rows * block) + 20 * size * block
    return pl.pallas_call(
        body,
        grid_spec=pltpu.PrefetchScalarGridSpec(
            num_scalar_prefetch=1,
            grid=(width // block,),
            in_specs=in_specs,
            out_specs=pl.BlockSpec((size, block), lambda i, table: (0, i)),
            scratch_shapes=[pltpu.VMEM((count, size, rows), jnp.bfloat16)],
        ),
        out_shape=jax.ShapeDtypeStruct((size, width), jnp.float32),
        name="down_step",
        compiler_params=pltpu.CompilerParams(vmem_limit_bytes=need + (1 << 20)),
        cost_estimate=pl.CostEstimate(
            flops=2 * count * rows * size * width,
            bytes_accessed=2 * count * rows * (size + width) + 8 * size * width,
            transcendentals=0,
        ),
    )(table, *operands)


def last_step(acc, pieces, weights, out_type):
    count = len(pieces)
    size, width = acc.shape
    block = min(width, 512)

    def body(*refs):
        piece_refs, weight_refs = refs[:count], refs[count : 2 * count]
        total_ref, out = refs[2 * count :]
        turned = [piece[...].T for piece in piece_refs]
        for at in range(0, width, block):
            columns = slice(at, at + block)
            total = total_ref[:, columns]
            for rows, weight in zip(turned, weight_refs):
                total = total + jnp.dot(
                    rows, weight[:, columns], preferred_element_type=jnp.float32
                )
            out[:, columns] = total.astype(out.dtype)

    flops = 2 * size * width * sum(piece.shape[0] for piece in pieces)
    return small_call(
        body,
        list(pieces) + list(weights) + [acc],
        jax.ShapeDtypeStruct((size, width), out_type),
        flops,
        limit=8,
    )


def token_slice(hidden, low, high):
    if low == 0 and high == hidden.shape[1]:
        return hidden

    parts = 8 if hidden.shape[0] % 64 == 0 else 1
    rows = hidden.shape[0] // parts

    def body(source, target, semaphores):
        copies = [
            pltpu.make_async_copy(
                source.at[j * rows : (j + 1) * rows, low:high],
                target.at[j * rows : (j + 1) * rows],
                semaphores.at[j],
            )
            for j in range(parts)
        ]
        for copy in copies:
            copy.start()
        for copy in copies:
            copy.wait()

    shape = (hidden.shape[0], high - low)
    return pl.pallas_call(
        body,
        in_specs=[pl.BlockSpec(memory_space=pltpu.HBM)],
        out_specs=IN_VMEM,
        out_shape=pltpu.VMEM(shape, hidden.dtype),
        scratch_shapes=[pltpu.SemaphoreType.DMA((parts,))],
        name="token_slice",
        compiler_params=pltpu.CompilerParams(vmem_limit_bytes=4 << 20),
        cost_estimate=pl.CostEstimate(
            flops=0, bytes_accessed=4 * shape[0] * shape[1], transcendentals=0
        ),
    )(pltpu.with_memory_space_constraint(hidden, pltpu.HBM))


def regrouped(table, source, picks, shape, pick_of):
    count = len(picks)

    def body(table_ref, source_ref, *refs):
        targets = refs[:count]
        buffers, arrive, leave = refs[count:]

        def load(j):
            block = source_ref.at[pick_of(table_ref, picks[j])]
            return pltpu.make_async_copy(block, buffers.at[j % 3], arrive.at[j % 3])

        def store(j):
            return pltpu.make_async_copy(buffers.at[j % 3], targets[j], leave.at[j % 3])

        for j in range(min(2, count)):
            load(j).start()
        for j in range(count):
            load(j).wait()
            store(j).start()
            if j + 2 < count:
                if j >= 1:
                    store(j - 1).wait()
                load(j + 2).start()
        for j in range(max(0, count - 3), count):
            store(j).wait()

    in_hbm = pl.BlockSpec(memory_space=pltpu.HBM)
    elements = count
    for extent in shape:
        elements *= extent
    return pl.pallas_call(
        body,
        in_specs=[IN_SMEM, in_hbm],
        out_specs=[in_hbm] * count,
        out_shape=[pltpu.HBM(shape, source.dtype)] * count,
        scratch_shapes=[
            pltpu.VMEM((3,) + shape, source.dtype),
            pltpu.SemaphoreType.DMA((3,)),
            pltpu.SemaphoreType.DMA((3,)),
        ],
        name="regrouped",
        compiler_params=pltpu.CompilerParams(vmem_limit_bytes=20 << 20),
        cost_estimate=pl.CostEstimate(flops=0, bytes_accessed=4 * elements, transcendentals=0),
    )(table, pltpu.with_memory_space_constraint(source, pltpu.HBM))


def small_call(body, operands, outs, flops, scratch=(), smem=0, limit=5):
    total = sum(x.size * x.dtype.itemsize for x in operands[smem:])
    single = not isinstance(outs, (list, tuple))
    return pl.pallas_call(
        body,
        in_specs=[IN_SMEM] * smem + [IN_VMEM] * (len(operands) - smem),
        out_specs=IN_VMEM if single else [IN_VMEM] * len(outs),
        out_shape=outs,
        scratch_shapes=list(scratch),
        compiler_params=pltpu.CompilerParams(vmem_limit_bytes=limit << 20),
        cost_estimate=pl.CostEstimate(flops=flops, bytes_accessed=total, transcendentals=0),
    )(*operands)


def finish(mine, theirs, res_t, low, gain_row, weights, columns, carry):
    size, width = mine.shape
    step = 16
    extra = ROOM if carry else 0

    def body(a, b, r, g, w, block, scaled, squares, shard, sums):
        @pl.loop(0, size // step, unroll=2)
        def _(i):
            rows = pl.ds(pl.multiple_of(i * step, step), step)
            res_rows = pl.ds(pl.multiple_of(i * step + low, step), step)
            both = a[rows, :].astype(jnp.float32) + b[rows, :].astype(jnp.float32)
            new = (r[res_rows, :].astype(jnp.float32) + both).astype(jnp.bfloat16)
            block[rows, :] = new
            value = new.astype(jnp.float32)
            scaled[rows, :] = (value * g[...]).astype(jnp.bfloat16)
            square = value * value
            sums[rows, :] = jnp.broadcast_to(
                jnp.sum(square, axis=1, keepdims=True), (step, LANES)
            )

        squares[...] = sums[...].T[:8]
        term = jnp.dot(scaled[...], w[...], preferred_element_type=jnp.float32)
        shard[:size, :] = term.astype(jnp.bfloat16)
        if carry:
            shard[size:, :] = carried(squares[...], columns)

    shapes = [
        jax.ShapeDtypeStruct((size, width), jnp.bfloat16),
        jax.ShapeDtypeStruct((size, width), jnp.bfloat16),
        jax.ShapeDtypeStruct((8, size), jnp.float32),
    ]
    shapes.append(pltpu.VMEM((size + extra, columns), jnp.bfloat16))
    return small_call(
        body,
        [mine, theirs, res_t, gain_row, weights],
        shapes,
        2 * size * width * columns,
        [pltpu.VMEM((size, LANES), jnp.float32)],
    )


def carried(total, columns):
    missing = columns - total.shape[1]
    if missing:
        total = jnp.concatenate([total, jnp.zeros((ROOM, missing), jnp.float32)], 1)
    high = total.astype(jnp.bfloat16).astype(jnp.float32)
    upper = lax.broadcasted_iota(jnp.int32, total.shape, 0) < ROOM // 2
    return jnp.where(upper, high, total - high).astype(jnp.bfloat16)


def uncarried(rows, count):
    both = rows.astype(jnp.float32)
    return (both + pltpu.roll(both, ROOM // 2, 0))[:, :count]


def hop(came, scaled, weights, squares, columns, carry):
    count = scaled.shape[0]
    first = came is None

    def body(*refs):
        came_ref = None if first else refs[0]
        x, w, q, out = refs[0 if first else 1 :]
        total = jnp.dot(x[...], w[...], preferred_element_type=jnp.float32)
        if not first:
            total = total + came_ref[:count, :].astype(jnp.float32)
        out[:count, :] = total.astype(jnp.bfloat16)
        if carry:
            sums = q[...]
            if not first:
                sums = sums + uncarried(came_ref[count:, :], count)
            out[count:, :] = carried(sums, columns)

    operands = ([] if first else [came]) + [scaled, weights, squares]
    shape = pltpu.VMEM((count + (ROOM if carry else 0), columns), jnp.bfloat16)
    return small_call(body, operands, shape, 2 * count * scaled.shape[1] * columns)


def own_term(scaled, weights, columns):
    def body(x, w, out):
        out[...] = jnp.dot(
            x[...], w[...], preferred_element_type=jnp.float32
        )

    size, width = scaled.shape
    shape = jax.ShapeDtypeStruct((size, columns), jnp.float32)
    return small_call(body, [scaled, weights], shape, 2 * size * width * columns)


def own_rows(low_index, blocks, own_width):
    def body(low_ref, *refs):
        at = pl.multiple_of(low_ref[0] * own_width, own_width)
        start = 0
        for ref in refs[:-1]:
            refs[-1][:, start : start + ref.shape[0]] = ref[:, pl.ds(at, own_width)].T
            start += ref.shape[0]

    tokens = sum(block.shape[0] for block in blocks)
    shape = jax.ShapeDtypeStruct((own_width, tokens), blocks[0].dtype)
    return small_call(body, [low_index.reshape(1)] + blocks, shape, 0, (), 1)


def last_sum(parts, carry):
    bounds = [0]
    for own, _, _, _ in parts:
        bounds.append(bounds[-1] + own.shape[0])
    tokens, columns = bounds[-1], parts[0][0].shape[1]

    def body(*refs):
        out, whole, sums = refs[-3:]
        for i, (low, high) in enumerate(zip(bounds, bounds[1:])):
            own, q, first, second = refs[4 * i : 4 * i + 4]
            count = high - low
            total = own[...] + first[:count, :].astype(jnp.float32)
            whole[low:high, :] = total + second[:count, :].astype(jnp.float32)
            square = q[...]
            if carry:
                square = square + uncarried(first[count:, :], count)
                square = square + uncarried(second[count:, :], count)
            sums[:, low:high] = square
        inverse = lax.rsqrt(sums[0:1, :] / D + 1e-05)
        out[...] = (whole[...].T * inverse).astype(jnp.bfloat16)

    return small_call(
        body,
        [array for part in parts for array in part],
        jax.ShapeDtypeStruct((columns, tokens), jnp.bfloat16),
        tokens * columns,
        [pltpu.VMEM((tokens, columns), jnp.float32), pltpu.VMEM((8, tokens), jnp.float32)],
    )


def on_device(hidden, residual, w_down, gain, w_qkv):
    dev_index = lax.axis_index("gx")
    ys = lax.axis_size("gx") // XS
    y_bits = ys.bit_length() - 1
    x_bits = XS.bit_length() - 1
    place = place_of(dev_index // ys)
    low_index = dev_index % ys
    table = block_at((place + jnp.arange(XS, dtype=jnp.int32)) % XS).astype(jnp.int32)

    chunk_rows, tokens = hidden.shape
    half_rows = chunk_rows // 2
    width = w_down.shape[2]
    own_width = residual.shape[0]
    columns = w_qkv.shape[2] // XS
    chunk_tiles = w_down.reshape(XS, chunk_rows, width)
    half_tiles = w_down.reshape(XS * 2, half_rows, width)
    qkv_tile = w_qkv[0]
    if columns % LANES:
        qkv_tile = qkv_tile.reshape(width, XS, columns).transpose(1, 0, 2)

    bounds = token_groups(tokens)

    ups, downs = [], []
    for low, high in bounds:
        own = token_slice(hidden, low, high)
        up, down = [own], [own]
        for step in range(1, FAR + 1):
            last = step == FAR
            up.append(moved(up[-1][:half_rows] if last else up[-1], ys, 1))
            down.append(moved(down[-1][half_rows:] if last else down[-1], ys, -1))
        ups.append(up)
        downs.append(down)

    res_t = residual.T
    gain_full = gain
    for position in range(y_bits):
        high = (dev_index >> position) % 2 == 1
        other_res = swapped(res_t, position)
        other_gain = swapped(gain_full, position)
        res_t = jnp.where(
            high,
            jnp.concatenate([other_res, res_t], 1),
            jnp.concatenate([res_t, other_res], 1),
        )
        gain_full = jnp.where(
            high,
            jnp.concatenate([other_gain, gain_full], 0),
            jnp.concatenate([gain_full, other_gain], 0),
        )
    gain_row = gain_full.astype(jnp.float32)[None, :]

    if columns % LANES:
        pick_of = lambda table_ref, distance: table_ref[distance]
    else:
        pick_of = lambda table_ref, distance: (
            slice(None),
            pl.ds(pl.multiple_of(table_ref[distance] * columns, LANES), columns),
        )
    weights = {}
    for far in ((4, 3, 5), (2, 6, 1), (7, 0)):
        blocks = regrouped(table, qkv_tile, far, (width, columns), pick_of)
        weights.update(zip(far, blocks))
    far_rows = regrouped(
        table,
        half_tiles,
        range(2),
        (half_rows, width),
        lambda table_ref, half: table_ref[FAR] * 2 + half,
    )

    near = FAR - 1
    acc = None
    for step in range(near):
        sides = [([up[step] for up in ups], -step), ([down[step] for down in downs], step)]
        acc = down_step(table, acc, 0, sides if step else sides[:1], chunk_tiles)
    sums = []
    for g, (low, high) in enumerate(bounds):
        sides = [([ups[g][near]], -near), ([downs[g][near]], near)]
        part = down_step(table, acc, low, sides, chunk_tiles)
        sums.append(last_step(part, [ups[g][FAR], downs[g][FAR]], far_rows, jnp.bfloat16))

    carry = columns >= max(high - low for low, high in bounds)
    blocks, parts = [], []
    for g, (low, high) in enumerate(bounds):
        mine = sums[g]
        for position in range(y_bits):
            theirs = swapped(mine, position)
            if position < y_bits - 1:
                mine = (mine.astype(jnp.float32) + theirs.astype(jnp.float32)).astype(jnp.bfloat16)
        block, scaled, squares, shard = finish(
            mine, theirs, res_t, low, gain_row, weights[FAR], columns, carry
        )
        blocks.append(block)
        far_way = 1 if g % 2 == 0 else -1
        came = []
        for by in (far_way, -far_way):
            held = None
            for distance in range(FAR if by == far_way else near, 0, -1):
                if distance == FAR:
                    held = shard
                else:
                    tile = weights[by * distance % XS]
                    held = hop(held, scaled, tile, squares, columns, carry)
                held = moved(held, ys, by)
            came.append(held)
        own_part = own_term(scaled, weights[0], columns)
        if not carry:
            for position in range(y_bits, y_bits + x_bits):
                squares = squares + swapped(squares, position)
        parts.append((own_part, squares, *came))
    stream = own_rows(low_index, blocks, own_width)
    qkv = last_sum(parts, carry)
    return (stream, qkv)


def solution(mesh):
    placed = (
        P("gx", "groups"),
        P("gx", "groups"),
        P("gx", None, None),
        P("gx"),
        P("gx", None, None),
    )
    return jax.shard_map(
        on_device,
        mesh=mesh,
        in_specs=placed,
        out_specs=(P("gx", "groups"), P("gx", "groups")),
        check_vma=False,
    )
```

```python
import jax
import jax.numpy as jnp
from jax import lax
from jax.experimental import pallas as pl
from jax.experimental.pallas import tpu as pltpu
from jax.sharding import PartitionSpec as P


D = 16384
XS = 8
FAR = XS // 2
LANES = 128
ROOM = 8


IN_VMEM = pl.BlockSpec(memory_space=pltpu.VMEM)
IN_SMEM = pl.BlockSpec(memory_space=pltpu.SMEM)


def block_at(place):
    return jnp.where(place < FAR, 2 * place, 2 * (XS - 1 - place) + 1)


def place_of(block):
    return jnp.where(block % 2 == 0, block // 2, XS - 1 - block // 2)


def static_block_at(place):
    return 2 * place if place < FAR else 2 * (XS - 1 - place) + 1


def moved(value, ys, by):
    route = []
    for place in range(XS):
        source = static_block_at(place)
        target = static_block_at((place + by) % XS)
        for low in range(ys):
            route.append((source * ys + low, target * ys + low))
    return lax.ppermute(value, "gx", route)


def swapped(value, stride):
    count = lax.axis_size("gx")
    return lax.ppermute(value, "gx", [(low, low ^ 1 << stride) for low in range(count)])


def token_groups(tokens):
    if tokens % (3 * LANES):
        return [(0, tokens)]
    return [(0, tokens * 2 // 3), (tokens * 2 // 3, tokens)]


def down_step(table, acc, low, sides, tiles):
    count, groups = len(sides), len(sides[0][0])
    rows, width = tiles.shape[1:]
    parts = tiles.shape[0] // XS
    widths = [piece.shape[1] for piece in sides[0][0]]
    size = sum(widths)
    block = min(width, 512)

    def body(table_ref, *refs):
        pieces, weights = refs[: count * groups], refs[count * groups : count * (groups + 1)]
        out, turned = refs[-2:]

        @pl.when(pl.program_id(0) == 0)
        def _():
            for j in range(count):
                start = 0
                for g in range(groups):
                    turned[j, start : start + widths[g], :] = pieces[j * groups + g][...].T
                    start += widths[g]

        total = None if acc is None else refs[count * (groups + 1)][...]
        for j in range(count):
            term = jnp.dot(turned[j], weights[j][0], preferred_element_type=jnp.float32)
            total = term if total is None else total + term
        out[...] = total

    def piece_spec(tokens):
        return pl.BlockSpec((rows, tokens), lambda i, table: (0, 0), pipeline_mode=pl.Buffered(1))

    def weight_spec(distance, part):
        at = distance % XS
        return pl.BlockSpec((1, rows, block), lambda i, table: (table[at] * parts + part, 0, i))

    in_specs = [piece_spec(tokens) for _ in sides for tokens in widths]
    in_specs += [weight_spec(far, part) for _, far, part in sides]
    operands = [piece for pieces, _, _ in sides for piece in pieces] + [tiles] * count
    if acc is not None:
        in_specs.append(pl.BlockSpec((size, block), lambda i, table: (low // size, i)))
        operands.append(acc)
    need = count * (4 * rows * size + 4 * rows * block) + 20 * size * block
    return pl.pallas_call(
        body,
        grid_spec=pltpu.PrefetchScalarGridSpec(
            num_scalar_prefetch=1,
            grid=(width // block,),
            in_specs=in_specs,
            out_specs=pl.BlockSpec((size, block), lambda i, table: (0, i)),
            scratch_shapes=[pltpu.VMEM((count, size, rows), jnp.bfloat16)],
        ),
        out_shape=jax.ShapeDtypeStruct((size, width), jnp.float32),
        name="down_step",
        compiler_params=pltpu.CompilerParams(vmem_limit_bytes=need + (1 << 20)),
        cost_estimate=pl.CostEstimate(
            flops=2 * count * rows * size * width,
            bytes_accessed=2 * count * rows * (size + width) + 8 * size * width,
            transcendentals=0,
        ),
    )(table, *operands)


def last_step(acc, pieces, weights, out_type):
    count = len(pieces)
    size, width = acc.shape
    block = min(width, 512)

    def body(*refs):
        piece_refs, weight_refs = refs[:count], refs[count : 2 * count]
        total_ref, out = refs[2 * count :]
        turned = [piece[...].T for piece in piece_refs]
        for at in range(0, width, block):
            columns = slice(at, at + block)
            total = total_ref[:, columns]
            for rows, weight in zip(turned, weight_refs):
                total = total + jnp.dot(
                    rows, weight[:, columns], preferred_element_type=jnp.float32
                )
            out[:, columns] = total.astype(out.dtype)

    flops = 2 * size * width * sum(piece.shape[0] for piece in pieces)
    return small_call(
        body,
        list(pieces) + list(weights) + [acc],
        jax.ShapeDtypeStruct((size, width), out_type),
        flops,
        limit=8,
    )


def token_slice(hidden, low, high):
    if low == 0 and high == hidden.shape[1]:
        return hidden

    parts = 8 if hidden.shape[0] % 64 == 0 else 1
    rows = hidden.shape[0] // parts

    def body(source, target, semaphores):
        copies = [
            pltpu.make_async_copy(
                source.at[j * rows : (j + 1) * rows, low:high],
                target.at[j * rows : (j + 1) * rows],
                semaphores.at[j],
            )
            for j in range(parts)
        ]
        for copy in copies:
            copy.start()
        for copy in copies:
            copy.wait()

    shape = (hidden.shape[0], high - low)
    return pl.pallas_call(
        body,
        in_specs=[pl.BlockSpec(memory_space=pltpu.HBM)],
        out_specs=IN_VMEM,
        out_shape=pltpu.VMEM(shape, hidden.dtype),
        scratch_shapes=[pltpu.SemaphoreType.DMA((parts,))],
        name="token_slice",
        compiler_params=pltpu.CompilerParams(vmem_limit_bytes=4 << 20),
        cost_estimate=pl.CostEstimate(
            flops=0, bytes_accessed=4 * shape[0] * shape[1], transcendentals=0
        ),
    )(pltpu.with_memory_space_constraint(hidden, pltpu.HBM))


def regrouped(table, source, picks, shape, pick_of):
    count = len(picks)

    def body(table_ref, source_ref, *refs):
        targets = refs[:count]
        buffers, arrive, leave = refs[count:]

        def load(j):
            block = source_ref.at[pick_of(table_ref, picks[j])]
            return pltpu.make_async_copy(block, buffers.at[j % 3], arrive.at[j % 3])

        def store(j):
            return pltpu.make_async_copy(buffers.at[j % 3], targets[j], leave.at[j % 3])

        for j in range(min(2, count)):
            load(j).start()
        for j in range(count):
            load(j).wait()
            store(j).start()
            if j + 2 < count:
                if j >= 1:
                    store(j - 1).wait()
                load(j + 2).start()
        for j in range(max(0, count - 3), count):
            store(j).wait()

    in_hbm = pl.BlockSpec(memory_space=pltpu.HBM)
    elements = count
    for extent in shape:
        elements *= extent
    return pl.pallas_call(
        body,
        in_specs=[IN_SMEM, in_hbm],
        out_specs=[in_hbm] * count,
        out_shape=[pltpu.HBM(shape, source.dtype)] * count,
        scratch_shapes=[
            pltpu.VMEM((3,) + shape, source.dtype),
            pltpu.SemaphoreType.DMA((3,)),
            pltpu.SemaphoreType.DMA((3,)),
        ],
        name="regrouped",
        compiler_params=pltpu.CompilerParams(vmem_limit_bytes=20 << 20),
        cost_estimate=pl.CostEstimate(flops=0, bytes_accessed=4 * elements, transcendentals=0),
    )(table, pltpu.with_memory_space_constraint(source, pltpu.HBM))


def small_call(body, operands, outs, flops, scratch=(), smem=0, limit=5):
    total = sum(x.size * x.dtype.itemsize for x in operands[smem:])
    single = not isinstance(outs, (list, tuple))
    return pl.pallas_call(
        body,
        in_specs=[IN_SMEM] * smem + [IN_VMEM] * (len(operands) - smem),
        out_specs=IN_VMEM if single else [IN_VMEM] * len(outs),
        out_shape=outs,
        scratch_shapes=list(scratch),
        compiler_params=pltpu.CompilerParams(vmem_limit_bytes=limit << 20),
        cost_estimate=pl.CostEstimate(flops=flops, bytes_accessed=total, transcendentals=0),
    )(*operands)


def finish(mine, theirs, res_t, low, gain_row, weights, columns, carry):
    size, width = mine.shape
    step = 16
    extra = ROOM if carry else 0

    def body(a, b, r, g, w, block, scaled, squares, shard, sums):
        @pl.loop(0, size // step, unroll=2)
        def _(i):
            rows = pl.ds(pl.multiple_of(i * step, step), step)
            res_rows = pl.ds(pl.multiple_of(i * step + low, step), step)
            both = a[rows, :].astype(jnp.float32) + b[rows, :].astype(jnp.float32)
            new = (r[res_rows, :].astype(jnp.float32) + both).astype(jnp.bfloat16)
            block[rows, :] = new
            value = new.astype(jnp.float32)
            scaled[rows, :] = (value * g[...]).astype(jnp.bfloat16)
            square = value * value
            sums[rows, :] = jnp.broadcast_to(
                jnp.sum(square, axis=1, keepdims=True), (step, LANES)
            )

        squares[...] = sums[...].T[:8]
        term = jnp.dot(scaled[...], w[...], preferred_element_type=jnp.float32)
        shard[:size, :] = term.astype(jnp.bfloat16)
        if carry:
            shard[size:, :] = carried(squares[...], columns)

    shapes = [
        jax.ShapeDtypeStruct((size, width), jnp.bfloat16),
        jax.ShapeDtypeStruct((size, width), jnp.bfloat16),
        jax.ShapeDtypeStruct((8, size), jnp.float32),
    ]
    shapes.append(pltpu.VMEM((size + extra, columns), jnp.bfloat16))
    return small_call(
        body,
        [mine, theirs, res_t, gain_row, weights],
        shapes,
        2 * size * width * columns,
        [pltpu.VMEM((size, LANES), jnp.float32)],
    )


def carried(total, columns):
    missing = columns - total.shape[1]
    if missing:
        total = jnp.concatenate([total, jnp.zeros((ROOM, missing), jnp.float32)], 1)
    high = total.astype(jnp.bfloat16).astype(jnp.float32)
    upper = lax.broadcasted_iota(jnp.int32, total.shape, 0) < ROOM // 2
    return jnp.where(upper, high, total - high).astype(jnp.bfloat16)


def uncarried(rows, count):
    both = rows.astype(jnp.float32)
    return (both + pltpu.roll(both, ROOM // 2, 0))[:, :count]


def hop(came, scaled, weights, squares, columns, carry):
    count = scaled.shape[0]
    first = came is None

    def body(*refs):
        came_ref = None if first else refs[0]
        x, w, q, out = refs[0 if first else 1 :]
        total = jnp.dot(x[...], w[...], preferred_element_type=jnp.float32)
        if not first:
            total = total + came_ref[:count, :].astype(jnp.float32)
        out[:count, :] = total.astype(jnp.bfloat16)
        if carry:
            sums = q[...]
            if not first:
                sums = sums + uncarried(came_ref[count:, :], count)
            out[count:, :] = carried(sums, columns)

    operands = ([] if first else [came]) + [scaled, weights, squares]
    shape = pltpu.VMEM((count + (ROOM if carry else 0), columns), jnp.bfloat16)
    return small_call(body, operands, shape, 2 * count * scaled.shape[1] * columns)


def own_term(scaled, weights, columns):
    def body(x, w, out):
        out[...] = jnp.dot(
            x[...], w[...], preferred_element_type=jnp.float32
        )

    size, width = scaled.shape
    shape = jax.ShapeDtypeStruct((size, columns), jnp.float32)
    return small_call(body, [scaled, weights], shape, 2 * size * width * columns)


def own_rows(low_index, blocks, own_width):
    def body(low_ref, *refs):
        at = pl.multiple_of(low_ref[0] * own_width, own_width)
        start = 0
        for ref in refs[:-1]:
            refs[-1][:, start : start + ref.shape[0]] = ref[:, pl.ds(at, own_width)].T
            start += ref.shape[0]

    tokens = sum(block.shape[0] for block in blocks)
    shape = jax.ShapeDtypeStruct((own_width, tokens), blocks[0].dtype)
    return small_call(body, [low_index.reshape(1)] + blocks, shape, 0, (), 1)


def last_sum(parts, carry):
    bounds = [0]
    for own, _, _, _ in parts:
        bounds.append(bounds[-1] + own.shape[0])
    tokens, columns = bounds[-1], parts[0][0].shape[1]

    def body(*refs):
        out, whole, sums = refs[-3:]
        for i, (low, high) in enumerate(zip(bounds, bounds[1:])):
            own, q, first, second = refs[4 * i : 4 * i + 4]
            count = high - low
            total = own[...] + first[:count, :].astype(jnp.float32)
            whole[low:high, :] = total + second[:count, :].astype(jnp.float32)
            square = q[...]
            if carry:
                square = square + uncarried(first[count:, :], count)
                square = square + uncarried(second[count:, :], count)
            sums[:, low:high] = square
        inverse = lax.rsqrt(sums[0:1, :] / D + 1e-05)
        out[...] = (whole[...].T * inverse).astype(jnp.bfloat16)

    return small_call(
        body,
        [array for part in parts for array in part],
        jax.ShapeDtypeStruct((columns, tokens), jnp.bfloat16),
        tokens * columns,
        [pltpu.VMEM((tokens, columns), jnp.float32), pltpu.VMEM((8, tokens), jnp.float32)],
    )


def on_device(hidden, residual, w_down, gain, w_qkv):
    dev_index = lax.axis_index("gx")
    ys = lax.axis_size("gx") // XS
    y_bits = ys.bit_length() - 1
    x_bits = XS.bit_length() - 1
    place = place_of(dev_index // ys)
    low_index = dev_index % ys
    table = block_at((place + jnp.arange(XS, dtype=jnp.int32)) % XS).astype(jnp.int32)

    chunk_rows, tokens = hidden.shape
    half_rows = chunk_rows // 2
    width = w_down.shape[2]
    own_width = residual.shape[0]
    columns = w_qkv.shape[2] // XS
    chunk_tiles = w_down.reshape(XS, chunk_rows, width)
    half_tiles = w_down.reshape(XS * 2, half_rows, width)
    qkv_tile = w_qkv[0]
    if columns % LANES:
        qkv_tile = qkv_tile.reshape(width, XS, columns).transpose(1, 0, 2)

    bounds = token_groups(tokens)

    near = FAR - 1
    split = len(bounds) > 1
    ups, downs = [], []
    for g, (low, high) in enumerate(bounds):
        own = token_slice(hidden, low, high)
        up, down = [own], [own]
        for step in range(1, FAR + 1):
            if step == near and split and g == 0:
                parts = {}
                for h in range(2):
                    rows = slice(h * half_rows, (h + 1) * half_rows)
                    parts["u", h] = moved(up[-1][rows], ys, 1)
                    parts["d", h] = moved(down[-1][rows], ys, -1)
                up.append((parts["u", 0], parts["u", 1]))
                down.append((parts["d", 0], parts["d", 1]))
                continue
            last = step == FAR
            if last:
                halves = isinstance(up[-1], tuple)
                up_sent = up[-1][0] if halves else up[-1][:half_rows]
                down_sent = down[-1][1] if halves else down[-1][half_rows:]
            else:
                up_sent, down_sent = up[-1], down[-1]
            up.append(moved(up_sent, ys, 1))
            down.append(moved(down_sent, ys, -1))
        ups.append(up)
        downs.append(down)

    res_t = residual.T
    gain_full = gain
    for position in range(y_bits):
        high = (dev_index >> position) % 2 == 1
        other_res = swapped(res_t, position)
        other_gain = swapped(gain_full, position)
        res_t = jnp.where(
            high,
            jnp.concatenate([other_res, res_t], 1),
            jnp.concatenate([res_t, other_res], 1),
        )
        gain_full = jnp.where(
            high,
            jnp.concatenate([other_gain, gain_full], 0),
            jnp.concatenate([gain_full, other_gain], 0),
        )
    gain_row = gain_full.astype(jnp.float32)[None, :]

    if columns % LANES:
        pick_of = lambda table_ref, distance: table_ref[distance]
    else:
        pick_of = lambda table_ref, distance: (
            slice(None),
            pl.ds(pl.multiple_of(table_ref[distance] * columns, LANES), columns),
        )
    weights = {}
    for far in ((4, 3, 5), (2, 6, 1), (7, 0)):
        blocks = regrouped(table, qkv_tile, far, (width, columns), pick_of)
        weights.update(zip(far, blocks))
    far_rows = regrouped(
        table,
        half_tiles,
        range(2),
        (half_rows, width),
        lambda table_ref, half: table_ref[FAR] * 2 + half,
    )

    acc = None
    for step in range(near):
        sides = [([up[step] for up in ups], -step, 0), ([down[step] for down in downs], step, 0)]
        acc = down_step(table, acc, 0, sides if step else sides[:1], chunk_tiles)
    sums = []
    for g, (low, high) in enumerate(bounds):
        up, down = ups[g][near], downs[g][near]
        if isinstance(up, tuple):
            part, start = acc, low
            for h in (0, 1):
                sides = [([up[h]], -near, h), ([down[1 - h]], near, 1 - h)]
                part = down_step(table, part, start, sides, half_tiles)
                start = 0
        else:
            sides = [([up], -near, 0), ([down], near, 0)]
            part = down_step(table, acc, low, sides, chunk_tiles)
        sums.append(last_step(part, [ups[g][FAR], downs[g][FAR]], far_rows, jnp.bfloat16))

    carry = columns >= max(high - low for low, high in bounds)
    blocks, parts = [], []
    for g, (low, high) in enumerate(bounds):
        mine = sums[g]
        for position in range(y_bits):
            theirs = swapped(mine, position)
            if position < y_bits - 1:
                mine = (mine.astype(jnp.float32) + theirs.astype(jnp.float32)).astype(jnp.bfloat16)
        block, scaled, squares, shard = finish(
            mine, theirs, res_t, low, gain_row, weights[FAR], columns, carry
        )
        blocks.append(block)
        far_way = 1 if g % 2 == 0 else -1
        came = []
        for by in (far_way, -far_way):
            held = None
            for distance in range(FAR if by == far_way else near, 0, -1):
                if distance == FAR:
                    held = shard
                else:
                    tile = weights[by * distance % XS]
                    held = hop(held, scaled, tile, squares, columns, carry)
                held = moved(held, ys, by)
            came.append(held)
        own_part = own_term(scaled, weights[0], columns)
        if not carry:
            for position in range(y_bits, y_bits + x_bits):
                squares = squares + swapped(squares, position)
        parts.append((own_part, squares, *came))
    stream = own_rows(low_index, blocks, own_width)
    qkv = last_sum(parts, carry)
    return (stream, qkv)


def solution(mesh):
    placed = (
        P("gx", "groups"),
        P("gx", "groups"),
        P("gx", None, None),
        P("gx"),
        P("gx", None, None),
    )
    return jax.shard_map(
        on_device,
        mesh=mesh,
        in_specs=placed,
        out_specs=(P("gx", "groups"), P("gx", "groups")),
        check_vma=False,
    )
```

```python
import jax
import jax.numpy as jnp
from jax import lax
from jax.experimental import pallas as pl
from jax.experimental.pallas import tpu as pltpu
from jax.sharding import PartitionSpec as P


D = 16384
XS = 8
FAR = XS // 2
LANES = 128
ROOM = 8


IN_VMEM = pl.BlockSpec(memory_space=pltpu.VMEM)
IN_SMEM = pl.BlockSpec(memory_space=pltpu.SMEM)


def block_at(place):
    return jnp.where(place < FAR, 2 * place, 2 * (XS - 1 - place) + 1)


def place_of(block):
    return jnp.where(block % 2 == 0, block // 2, XS - 1 - block // 2)


def static_block_at(place):
    return 2 * place if place < FAR else 2 * (XS - 1 - place) + 1


def moved(value, ys, by):
    route = []
    for place in range(XS):
        source = static_block_at(place)
        target = static_block_at((place + by) % XS)
        for low in range(ys):
            route.append((source * ys + low, target * ys + low))
    return lax.ppermute(value, "gx", route)


def swapped(value, stride):
    count = lax.axis_size("gx")
    return lax.ppermute(value, "gx", [(low, low ^ 1 << stride) for low in range(count)])


def token_groups(tokens):
    if tokens % (3 * LANES):
        return [(0, tokens)]
    return [(0, tokens * 2 // 3), (tokens * 2 // 3, tokens)]


def down_step(table, acc, low, sides, tiles):
    count, groups = len(sides), len(sides[0][0])
    rows, width = tiles.shape[1:]
    parts = tiles.shape[0] // XS
    widths = [piece.shape[1] for piece in sides[0][0]]
    size = sum(widths)
    block = min(width, 512)

    def body(table_ref, *refs):
        pieces, weights = refs[: count * groups], refs[count * groups : count * (groups + 1)]
        out, turned = refs[-2:]

        @pl.when(pl.program_id(0) == 0)
        def _():
            for j in range(count):
                start = 0
                for g in range(groups):
                    turned[j, start : start + widths[g], :] = pieces[j * groups + g][...].T
                    start += widths[g]

        total = None if acc is None else refs[count * (groups + 1)][...]
        for j in range(count):
            term = jnp.dot(turned[j], weights[j][0], preferred_element_type=jnp.float32)
            total = term if total is None else total + term
        out[...] = total

    def piece_spec(tokens):
        return pl.BlockSpec((rows, tokens), lambda i, table: (0, 0), pipeline_mode=pl.Buffered(1))

    def weight_spec(distance, part):
        at = distance % XS
        return pl.BlockSpec((1, rows, block), lambda i, table: (table[at] * parts + part, 0, i))

    in_specs = [piece_spec(tokens) for _ in sides for tokens in widths]
    in_specs += [weight_spec(far, part) for _, far, part in sides]
    operands = [piece for pieces, _, _ in sides for piece in pieces] + [tiles] * count
    if acc is not None:
        in_specs.append(pl.BlockSpec((size, block), lambda i, table: (low // size, i)))
        operands.append(acc)
    need = count * (4 * rows * size + 4 * rows * block) + 20 * size * block
    return pl.pallas_call(
        body,
        grid_spec=pltpu.PrefetchScalarGridSpec(
            num_scalar_prefetch=1,
            grid=(width // block,),
            in_specs=in_specs,
            out_specs=pl.BlockSpec((size, block), lambda i, table: (0, i)),
            scratch_shapes=[pltpu.VMEM((count, size, rows), jnp.bfloat16)],
        ),
        out_shape=jax.ShapeDtypeStruct((size, width), jnp.float32),
        name="down_step",
        compiler_params=pltpu.CompilerParams(vmem_limit_bytes=need + (1 << 20)),
        cost_estimate=pl.CostEstimate(
            flops=2 * count * rows * size * width,
            bytes_accessed=2 * count * rows * (size + width) + 8 * size * width,
            transcendentals=0,
        ),
    )(table, *operands)


def last_step(acc, low, pieces, weights, out_type, limit):
    count = len(pieces)
    flat = [weight for several in weights for weight in several]
    owner = [(j, i) for j, several in enumerate(weights) for i in range(len(several))]
    size, width = pieces[0].shape[1], acc.shape[1]
    rows = flat[0].shape[0]
    block = min(width, 512)

    def body(*refs):
        piece_refs, weight_refs = refs[:count], refs[count : count + len(flat)]
        total_ref, out = refs[count + len(flat) :]
        turned = [piece_refs[j][i * rows : (i + 1) * rows, :].T for j, i in owner]
        for at in range(0, width, block):
            columns = slice(at, at + block)
            total = total_ref[low : low + size, columns]
            for part, weight in zip(turned, weight_refs):
                total = total + jnp.dot(
                    part, weight[:, columns], preferred_element_type=jnp.float32
                )
            out[:, columns] = total.astype(out.dtype)

    return small_call(
        body,
        list(pieces) + flat + [acc],
        jax.ShapeDtypeStruct((size, width), out_type),
        2 * size * width * rows * len(flat),
        limit=limit,
    )


def token_slice(hidden, low, high):
    if low == 0 and high == hidden.shape[1]:
        return hidden

    parts = 8 if hidden.shape[0] % 64 == 0 else 1
    rows = hidden.shape[0] // parts

    def body(source, target, semaphores):
        copies = [
            pltpu.make_async_copy(
                source.at[j * rows : (j + 1) * rows, low:high],
                target.at[j * rows : (j + 1) * rows],
                semaphores.at[j],
            )
            for j in range(parts)
        ]
        for copy in copies:
            copy.start()
        for copy in copies:
            copy.wait()

    shape = (hidden.shape[0], high - low)
    return pl.pallas_call(
        body,
        in_specs=[pl.BlockSpec(memory_space=pltpu.HBM)],
        out_specs=IN_VMEM,
        out_shape=pltpu.VMEM(shape, hidden.dtype),
        scratch_shapes=[pltpu.SemaphoreType.DMA((parts,))],
        name="token_slice",
        compiler_params=pltpu.CompilerParams(vmem_limit_bytes=4 << 20),
        cost_estimate=pl.CostEstimate(
            flops=0, bytes_accessed=4 * shape[0] * shape[1], transcendentals=0
        ),
    )(pltpu.with_memory_space_constraint(hidden, pltpu.HBM))


def regrouped(table, source, picks, shape, pick_of):
    count = len(picks)

    def body(table_ref, source_ref, *refs):
        targets = refs[:count]
        buffers, arrive, leave = refs[count:]

        def load(j):
            block = source_ref.at[pick_of(table_ref, picks[j])]
            return pltpu.make_async_copy(block, buffers.at[j % 3], arrive.at[j % 3])

        def store(j):
            return pltpu.make_async_copy(buffers.at[j % 3], targets[j], leave.at[j % 3])

        for j in range(min(2, count)):
            load(j).start()
        for j in range(count):
            load(j).wait()
            store(j).start()
            if j + 2 < count:
                if j >= 1:
                    store(j - 1).wait()
                load(j + 2).start()
        for j in range(max(0, count - 3), count):
            store(j).wait()

    in_hbm = pl.BlockSpec(memory_space=pltpu.HBM)
    elements = count
    for extent in shape:
        elements *= extent
    return pl.pallas_call(
        body,
        in_specs=[IN_SMEM, in_hbm],
        out_specs=[in_hbm] * count,
        out_shape=[pltpu.HBM(shape, source.dtype)] * count,
        scratch_shapes=[
            pltpu.VMEM((3,) + shape, source.dtype),
            pltpu.SemaphoreType.DMA((3,)),
            pltpu.SemaphoreType.DMA((3,)),
        ],
        name="regrouped",
        compiler_params=pltpu.CompilerParams(vmem_limit_bytes=20 << 20),
        cost_estimate=pl.CostEstimate(flops=0, bytes_accessed=4 * elements, transcendentals=0),
    )(table, pltpu.with_memory_space_constraint(source, pltpu.HBM))


def small_call(body, operands, outs, flops, scratch=(), smem=0, limit=5):
    total = sum(x.size * x.dtype.itemsize for x in operands[smem:])
    single = not isinstance(outs, (list, tuple))
    return pl.pallas_call(
        body,
        in_specs=[IN_SMEM] * smem + [IN_VMEM] * (len(operands) - smem),
        out_specs=IN_VMEM if single else [IN_VMEM] * len(outs),
        out_shape=outs,
        scratch_shapes=list(scratch),
        compiler_params=pltpu.CompilerParams(vmem_limit_bytes=limit << 20),
        cost_estimate=pl.CostEstimate(flops=flops, bytes_accessed=total, transcendentals=0),
    )(*operands)


def finish(mine, theirs, res_t, low, gain_row, weights, columns, carry):
    size, width = mine.shape
    step = 16
    extra = ROOM if carry else 0

    def body(a, b, r, g, w, block, scaled, squares, shard, sums):
        @pl.loop(0, size // step, unroll=2)
        def _(i):
            rows = pl.ds(pl.multiple_of(i * step, step), step)
            res_rows = pl.ds(pl.multiple_of(i * step + low, step), step)
            both = a[rows, :].astype(jnp.float32) + b[rows, :].astype(jnp.float32)
            new = (r[res_rows, :].astype(jnp.float32) + both).astype(jnp.bfloat16)
            block[rows, :] = new
            value = new.astype(jnp.float32)
            scaled[rows, :] = (value * g[...]).astype(jnp.bfloat16)
            square = value * value
            sums[rows, :] = jnp.broadcast_to(
                jnp.sum(square, axis=1, keepdims=True), (step, LANES)
            )

        squares[...] = sums[...].T[:8]
        term = jnp.dot(scaled[...], w[...], preferred_element_type=jnp.float32)
        shard[:size, :] = term.astype(jnp.bfloat16)
        if carry:
            shard[size:, :] = carried(squares[...], columns)

    shapes = [
        jax.ShapeDtypeStruct((size, width), jnp.bfloat16),
        jax.ShapeDtypeStruct((size, width), jnp.bfloat16),
        jax.ShapeDtypeStruct((8, size), jnp.float32),
    ]
    shapes.append(pltpu.VMEM((size + extra, columns), jnp.bfloat16))
    return small_call(
        body,
        [mine, theirs, res_t, gain_row, weights],
        shapes,
        2 * size * width * columns,
        [pltpu.VMEM((size, LANES), jnp.float32)],
    )


def carried(total, columns):
    missing = columns - total.shape[1]
    if missing:
        total = jnp.concatenate([total, jnp.zeros((ROOM, missing), jnp.float32)], 1)
    high = total.astype(jnp.bfloat16).astype(jnp.float32)
    upper = lax.broadcasted_iota(jnp.int32, total.shape, 0) < ROOM // 2
    return jnp.where(upper, high, total - high).astype(jnp.bfloat16)


def uncarried(rows, count):
    both = rows.astype(jnp.float32)
    return (both + pltpu.roll(both, ROOM // 2, 0))[:, :count]


def hop(came, scaled, weights, squares, columns, carry):
    count = scaled.shape[0]
    first = came is None

    def body(*refs):
        came_ref = None if first else refs[0]
        x, w, q, out = refs[0 if first else 1 :]
        total = jnp.dot(x[...], w[...], preferred_element_type=jnp.float32)
        if not first:
            total = total + came_ref[:count, :].astype(jnp.float32)
        out[:count, :] = total.astype(jnp.bfloat16)
        if carry:
            sums = q[...]
            if not first:
                sums = sums + uncarried(came_ref[count:, :], count)
            out[count:, :] = carried(sums, columns)

    operands = ([] if first else [came]) + [scaled, weights, squares]
    shape = pltpu.VMEM((count + (ROOM if carry else 0), columns), jnp.bfloat16)
    return small_call(body, operands, shape, 2 * count * scaled.shape[1] * columns)


def own_term(scaled, weights, columns):
    def body(x, w, out):
        out[...] = jnp.dot(
            x[...], w[...], preferred_element_type=jnp.float32
        )

    size, width = scaled.shape
    shape = jax.ShapeDtypeStruct((size, columns), jnp.float32)
    return small_call(body, [scaled, weights], shape, 2 * size * width * columns)


def own_rows(low_index, blocks, own_width):
    def body(low_ref, *refs):
        at = pl.multiple_of(low_ref[0] * own_width, own_width)
        start = 0
        for ref in refs[:-1]:
            refs[-1][:, start : start + ref.shape[0]] = ref[:, pl.ds(at, own_width)].T
            start += ref.shape[0]

    tokens = sum(block.shape[0] for block in blocks)
    shape = jax.ShapeDtypeStruct((own_width, tokens), blocks[0].dtype)
    return small_call(body, [low_index.reshape(1)] + blocks, shape, 0, (), 1)


def last_sum(parts, carry):
    bounds = [0]
    for own, _, _, _ in parts:
        bounds.append(bounds[-1] + own.shape[0])
    tokens, columns = bounds[-1], parts[0][0].shape[1]

    def body(*refs):
        out, whole, sums = refs[-3:]
        for i, (low, high) in enumerate(zip(bounds, bounds[1:])):
            own, q, first, second = refs[4 * i : 4 * i + 4]
            count = high - low
            total = own[...] + first[:count, :].astype(jnp.float32)
            whole[low:high, :] = total + second[:count, :].astype(jnp.float32)
            square = q[...]
            if carry:
                square = square + uncarried(first[count:, :], count)
                square = square + uncarried(second[count:, :], count)
            sums[:, low:high] = square
        inverse = lax.rsqrt(sums[0:1, :] / D + 1e-05)
        out[...] = (whole[...].T * inverse).astype(jnp.bfloat16)

    return small_call(
        body,
        [array for part in parts for array in part],
        jax.ShapeDtypeStruct((columns, tokens), jnp.bfloat16),
        tokens * columns,
        [pltpu.VMEM((tokens, columns), jnp.float32), pltpu.VMEM((8, tokens), jnp.float32)],
    )


def on_device(hidden, residual, w_down, gain, w_qkv):
    dev_index = lax.axis_index("gx")
    ys = lax.axis_size("gx") // XS
    y_bits = ys.bit_length() - 1
    x_bits = XS.bit_length() - 1
    place = place_of(dev_index // ys)
    low_index = dev_index % ys
    table = block_at((place + jnp.arange(XS, dtype=jnp.int32)) % XS).astype(jnp.int32)

    chunk_rows, tokens = hidden.shape
    half_rows = chunk_rows // 2
    width = w_down.shape[2]
    own_width = residual.shape[0]
    columns = w_qkv.shape[2] // XS
    chunk_tiles = w_down.reshape(XS, chunk_rows, width)
    half_tiles = w_down.reshape(XS * 2, half_rows, width)
    qkv_tile = w_qkv[0]
    if columns % LANES:
        qkv_tile = qkv_tile.reshape(width, XS, columns).transpose(1, 0, 2)

    bounds = token_groups(tokens)

    near = FAR - 1
    split = len(bounds) > 1
    ups, downs = [], []
    for g, (low, high) in enumerate(bounds):
        own = token_slice(hidden, low, high)
        up, down = [own], [own]
        for step in range(1, FAR + 1):
            if step == near and split and g == 0:
                parts = {}
                for h in range(2):
                    rows = slice(h * half_rows, (h + 1) * half_rows)
                    parts["u", h] = moved(up[-1][rows], ys, 1)
                    parts["d", h] = moved(down[-1][rows], ys, -1)
                up.append((parts["u", 0], parts["u", 1]))
                down.append((parts["d", 0], parts["d", 1]))
                continue
            last = step == FAR
            if last:
                halves = isinstance(up[-1], tuple)
                up_sent = up[-1][0] if halves else up[-1][:half_rows]
                down_sent = down[-1][1] if halves else down[-1][half_rows:]
            else:
                up_sent, down_sent = up[-1], down[-1]
            up.append(moved(up_sent, ys, 1))
            down.append(moved(down_sent, ys, -1))
        ups.append(up)
        downs.append(down)

    res_t = residual.T
    gain_full = gain
    for position in range(y_bits):
        high = (dev_index >> position) % 2 == 1
        other_res = swapped(res_t, position)
        other_gain = swapped(gain_full, position)
        res_t = jnp.where(
            high,
            jnp.concatenate([other_res, res_t], 1),
            jnp.concatenate([res_t, other_res], 1),
        )
        gain_full = jnp.where(
            high,
            jnp.concatenate([other_gain, gain_full], 0),
            jnp.concatenate([gain_full, other_gain], 0),
        )
    gain_row = gain_full.astype(jnp.float32)[None, :]

    if columns % LANES:
        pick_of = lambda table_ref, distance: table_ref[distance]
    else:
        pick_of = lambda table_ref, distance: (
            slice(None),
            pl.ds(pl.multiple_of(table_ref[distance] * columns, LANES), columns),
        )
    weights = {}
    for far in ((4, 3, 5), (2, 6, 1), (7, 0)):
        blocks = regrouped(table, qkv_tile, far, (width, columns), pick_of)
        weights.update(zip(far, blocks))
    near_rows = []
    if split:
        for distance in (XS - near, near):
            near_rows.append(
                regrouped(
                    table,
                    half_tiles,
                    [(distance, h) for h in range(2)],
                    (half_rows, width),
                    lambda table_ref, pick: table_ref[pick[0]] * 2 + pick[1],
                )
            )
    far_rows = regrouped(
        table,
        half_tiles,
        range(2),
        (half_rows, width),
        lambda table_ref, half: table_ref[FAR] * 2 + half,
    )

    acc = None
    for step in range(near):
        sides = [([up[step] for up in ups], -step, 0), ([down[step] for down in downs], step, 0)]
        acc = down_step(table, acc, 0, sides if step else sides[:1], chunk_tiles)
    sums = []
    for g, (low, high) in enumerate(bounds):
        up, down = ups[g][near], downs[g][near]
        if isinstance(up, tuple):
            part, start = acc, low
            for h in (0, 1):
                sides = [([up[h]], -near, h), ([down[1 - h]], near, 1 - h)]
                part = down_step(table, part, start, sides, half_tiles)
                start = 0
        elif split:
            part = last_step(acc, low, [up, down], near_rows, jnp.float32, 8)
        else:
            sides = [([up], -near, 0), ([down], near, 0)]
            part = down_step(table, acc, low, sides, chunk_tiles)
        sides = [ups[g][FAR], downs[g][FAR]]
        sums.append(last_step(part, 0, sides, [[w] for w in far_rows], jnp.bfloat16, 8))

    carry = columns >= max(high - low for low, high in bounds)
    blocks, parts = [], []
    for g, (low, high) in enumerate(bounds):
        mine = sums[g]
        for position in range(y_bits):
            theirs = swapped(mine, position)
            if position < y_bits - 1:
                mine = (mine.astype(jnp.float32) + theirs.astype(jnp.float32)).astype(jnp.bfloat16)
        block, scaled, squares, shard = finish(
            mine, theirs, res_t, low, gain_row, weights[FAR], columns, carry
        )
        blocks.append(block)
        far_way = 1 if g % 2 == 0 else -1
        came = []
        for by in (far_way, -far_way):
            held = None
            for distance in range(FAR if by == far_way else near, 0, -1):
                if distance == FAR:
                    held = shard
                else:
                    tile = weights[by * distance % XS]
                    held = hop(held, scaled, tile, squares, columns, carry)
                held = moved(held, ys, by)
            came.append(held)
        own_part = own_term(scaled, weights[0], columns)
        if not carry:
            for position in range(y_bits, y_bits + x_bits):
                squares = squares + swapped(squares, position)
        parts.append((own_part, squares, *came))
    stream = own_rows(low_index, blocks, own_width)
    qkv = last_sum(parts, carry)
    return (stream, qkv)


def solution(mesh):
    placed = (
        P("gx", "groups"),
        P("gx", "groups"),
        P("gx", None, None),
        P("gx"),
        P("gx", None, None),
    )
    return jax.shard_map(
        on_device,
        mesh=mesh,
        in_specs=placed,
        out_specs=(P("gx", "groups"), P("gx", "groups")),
        check_vma=False,
    )
```
